32 devices in a mesh: coil: 4 (over y, x), slab: 8 (over z, core).
Axes of the slice: x: 2, y: 2, z: 4, core: 2. Of those that a mesh axis runs over, the one named last changes fastest.
Arguments:
- coil_maps: float32 [8, 2, 8, 256, 128], P('coil', None, 'slab'), may hold values from -1.5 to 1.5
- kspace: float32 [8, 2, 8, 256, 128], P('coil', None, 'slab'), may hold values from -6 to 6
- sample_mask: int32 [256, 128], replicated, may hold values 0 or 1
- iterate: float32 [2, 8, 256, 128], P(None, 'slab', 'coil'), may hold values from -6 to 6
- probe_bits: int32 [2, 8, 256, 128], P(None, 'slab', 'coil'), may hold values from 0 to 1
- loss_gradient: float32 [2, 8, 256, 128], P(None, 'slab', 'coil'), may hold values from -6 to 6
- adjoint: float32 [2, 8, 256, 128], P(None, 'slab', 'coil'), may hold values from -6 to 6
- kernel_first: bfloat16 [24, 2, 3, 3, 3], replicated, may hold values from -0.875 to 0.875
- kernel_second: bfloat16 [24, 24, 3, 3, 3], replicated, may hold values from -0.25 to 0.25
- kernel_last: bfloat16 [2, 24, 3, 3, 3], replicated, may hold values from -0.25 to 0.25
Outputs:
- new_iterate: float32 [2, 8, 256, 128], P(None, 'slab', 'coil')
- probe_pullback: float32 [2, 8, 256, 128], P(None, 'slab', 'coil')
- adjoint_next: float32 [2, 8, 256, 128], P(None, 'slab', 'coil')
The draws below stay inside these ranges and needn't reach their ends.
Inputs may be any that keep to these rules, and one draw needn't show every extreme that they name: `sample_mask`: 1 marks a sampled phase-encode line. `probe_bits`: the probe's sign is 2 p - 1.
All inputs are finite; a program needn't handle non-finite values.
Results may differ from the reference program's by a relative error of at most 0.0055.
Values may be sent and summed in bfloat16 or wider, within the bound.
A program may use at most 128 MiB of HBM per device.

```python
import jax
import jax.numpy as jnp
from jax import lax

NC = 8
NY = 256
NZ = 128
CH = 24
NX = 8


def with_ends(entries, own_key, least, largest):
    shape = entries.shape
    place = [jax.random.randint(jax.random.fold_in(own_key, axis), (), 0, shape[axis]) for axis in range(len(shape))]
    entries = entries.at[tuple(place)].set(least)
    longest = shape.index(max(shape))
    place[longest] = (place[longest] + 1) % shape[longest]
    return entries.at[tuple(place)].set(largest)


def shard_levels(key, shape, pieces, low, high):
    factor_of = 1.0
    for axis_at, parts in pieces:
        heights = jax.random.uniform(jax.random.fold_in(jax.random.fold_in(key, 6), axis_at), (parts,), jnp.float32, low / len(pieces), high / len(pieces))
        factor_of = factor_of * jnp.repeat(jnp.exp(heights), shape[axis_at] // parts).reshape((-1,) + (1,) * (len(shape) - 1 - axis_at))
    return factor_of


def normal_values(stream_key, dims, deviation, bound, pieces=(), kind=jnp.bfloat16):
    values = deviation * jax.random.normal(stream_key, dims, jnp.float32)
    if pieces:
        values = values * shard_levels(stream_key, dims, pieces, -0.22, 0.18)
    return jnp.clip(values, -bound, bound).astype(kind)


def setup_inputs(seed: int = 0) -> dict:
    arg_keys = jax.random.split(jax.random.key(seed), 11)
    coil_maps = normal_values(arg_keys[0], (NC, 2, NX, NY, NZ), (2 * NC) ** -0.5, 1.5, ((0, 4), (2, 8)), jnp.float32)
    kspace = normal_values(arg_keys[1], (NC, 2, NX, NY, NZ), 1.0, 6.0, ((0, 4), (2, 8)), jnp.float32)
    sample_mask = with_ends((jax.random.randint(arg_keys[2], (NY, NZ), 0, 3) < 1).astype(jnp.int32), jax.random.fold_in(arg_keys[2], 1), 0, 1)
    iterate = normal_values(arg_keys[3], (2, NX, NY, NZ), 1.0, 6.0, ((1, 8), (2, 4)), jnp.float32)
    probe_bits = with_ends(jax.random.randint(arg_keys[4], (2, NX, NY, NZ), 0, 2), jax.random.fold_in(arg_keys[4], 1), 0, 1).astype(jnp.int32)
    loss_gradient = normal_values(arg_keys[5], (2, NX, NY, NZ), 1.0, 6.0, ((1, 8), (2, 4)), jnp.float32)
    adjoint = normal_values(arg_keys[6], (2, NX, NY, NZ), 1.0, 6.0, ((1, 8), (2, 4)), jnp.float32)
    kernel_first = normal_values(arg_keys[7], (CH, 2, 3, 3, 3), 54 ** -0.5, 0.875)
    kernel_second = normal_values(arg_keys[8], (CH, CH, 3, 3, 3), (27 * CH) ** -0.5, 0.25)
    kernel_last = normal_values(arg_keys[9], (2, CH, 3, 3, 3), (27 * CH) ** -0.5, 0.25)
    return {"coil_maps": coil_maps, "kspace": kspace, "sample_mask": sample_mask, "iterate": iterate, "probe_bits": probe_bits, "loss_gradient": loss_gradient, "adjoint": adjoint, "kernel_first": kernel_first, "kernel_second": kernel_second, "kernel_last": kernel_last}


step_size = 0.8
kernel_layout = ("NCDHW", "OIDHW", "NCDHW")


def spectrum(real_part, imag_part, inverse):
    joined = lax.complex(real_part, imag_part)
    if inverse:
        turned = jnp.fft.ifft2(joined, axes=(-2, -1), norm="ortho")
    else:
        turned = jnp.fft.fft2(joined, axes=(-2, -1), norm="ortho")
    return jnp.real(turned), jnp.imag(turned)


def coil_term(field, coil_map, mask_weight, data):
    field_real = field[:, 0]
    field_imag = field[:, 1]
    map_real = coil_map[0]
    map_imag = coil_map[1]
    coil_real = map_real * field_real - map_imag * field_imag
    coil_imag = map_real * field_imag + map_imag * field_real
    freq_real, freq_imag = spectrum(coil_real, coil_imag, False)
    freq_real = mask_weight * freq_real
    freq_imag = mask_weight * freq_imag
    if data is not None:
        freq_real = freq_real - mask_weight * data[0]
        freq_imag = freq_imag - mask_weight * data[1]
    back_real, back_imag = spectrum(freq_real, freq_imag, True)
    return jnp.stack([map_real * back_real + map_imag * back_imag,
                      map_real * back_imag - map_imag * back_real], axis=1)


def normal_sum(field, coil_maps, kspace, mask_weight, with_data):
    def coil_step(running, coil_index):
        data = kspace[coil_index] if with_data else None
        return running + coil_term(field, coil_maps[coil_index], mask_weight, data), None

    running, unused = lax.scan(coil_step, jnp.zeros(field.shape, jnp.float32),
                               jnp.arange(NC, dtype=jnp.int32))
    return running


def convolve(activation, kernel):
    return lax.conv_general_dilated(activation, kernel, (1, 1, 1), "SAME",
                                    dimension_numbers=kernel_layout,
                                    preferred_element_type=jnp.float32)


def transposed(kernel):
    return jnp.swapaxes(jnp.flip(kernel, (2, 3, 4)), 0, 1)


def silu_slope(preact):
    sigmoid_value = jax.nn.sigmoid(preact)
    return sigmoid_value * (1.0 + preact * (1.0 - sigmoid_value))


def reference(coil_maps, kspace, sample_mask, iterate, probe_bits, loss_gradient, adjoint,
              kernel_first, kernel_second, kernel_last):
    mask_weight = sample_mask.astype(jnp.float32)
    gradient = normal_sum(iterate[None], coil_maps, kspace, mask_weight, True)[0]
    relaxed = iterate - step_size * gradient
    activation = relaxed.astype(jnp.bfloat16)[None]
    preacts = []
    for kernel in (kernel_first, kernel_second):
        preact = convolve(activation, kernel)
        preacts.append(preact)
        activation = jax.nn.silu(preact).astype(jnp.bfloat16)
    new_iterate = relaxed + convolve(activation, kernel_last)[0]

    def pullback(cotangent):
        grad_field = convolve(cotangent.astype(jnp.bfloat16)[None], transposed(kernel_last))
        for kernel, preact in ((kernel_second, preacts[1]), (kernel_first, preacts[0])):
            grad_field = (grad_field * silu_slope(preact)).astype(jnp.bfloat16)
            grad_field = convolve(grad_field, transposed(kernel))
        return cotangent + grad_field[0]

    sign_field = (2 * probe_bits - 1).astype(jnp.float32)
    pulled = jnp.stack([pullback(sign_field), pullback(adjoint)])
    result = pulled - step_size * normal_sum(pulled, coil_maps, kspace, mask_weight, False)
    return new_iterate, result[0], loss_gradient + result[1]
```

```python
import math

import jax
import jax.numpy as jnp
import numpy as np
from jax import lax
from jax.experimental import pallas as pl
from jax.experimental.pallas import tpu as pltpu
from jax.sharding import PartitionSpec as P

step_size = 0.8
reach = 4
both = ("coil", "slab")
f32 = jnp.float32
bf16 = jnp.bfloat16
vmem = pl.BlockSpec(memory_space=pltpu.VMEM)
MESH = pl.DeviceIdType.MESH


def exchange(items, collective_id):
    coils, slabs = lax.axis_size("coil"), lax.axis_size("slab")
    count = len(items)
    sizes = [math.prod(lax.axis_size(a) for a in axes) for _, axes, _ in items]
    outs = []
    for (array, _, how), size in zip(items, sizes):
        tail = array.shape if how == "all" else array.shape[1:]
        outs.append(jax.ShapeDtypeStruct((size,) + tail, array.dtype))
    widest = items[int(np.argmax(sizes))][1]

    def kernel(*refs):
        sources, targets = refs[:count], refs[count : 2 * count]
        send_sems, recv_sems = refs[2 * count : 3 * count], refs[3 * count :]
        my_coil, my_slab = lax.axis_index("coil"), lax.axis_index("slab")

        def place(axes, rank):
            if axes == both:
                return lax.div(rank, slabs), lax.rem(rank, slabs)
            return (rank, my_slab) if axes == ("coil",) else (my_coil, rank)

        def my_rank(axes):
            if axes == both:
                return my_coil * slabs + my_slab
            return my_coil if axes == ("coil",) else my_slab

        def row(item, rank):
            if items[item][2] == "all":
                return sources[item]
            if items[item][2] == "slab":
                return sources[item].at[place(items[item][1], rank)[1]]
            return sources[item].at[rank]

        barrier = pltpu.get_barrier_semaphore()
        reached = max(sizes)

        def greet(step, carry):
            rank = lax.rem(my_rank(widest) + step, reached)
            pl.semaphore_signal(barrier, inc=1, device_id=place(widest, rank), device_id_type=MESH)
            return carry

        lax.fori_loop(1, reached, greet, 0)
        pl.semaphore_wait(barrier, reached - 1)

        def copy(item, step):
            axes, size = items[item][1], sizes[item]
            mine = my_rank(axes)
            rank = lax.rem(mine + step, size)
            return pltpu.make_async_remote_copy(
                src_ref=row(item, rank),
                dst_ref=targets[item].at[mine],
                send_sem=send_sems[item].at[step],
                recv_sem=recv_sems[item].at[step],
                device_id=place(axes, rank),
                device_id_type=MESH,
            )

        for item in range(count):
            lax.fori_loop(1, sizes[item], lambda s, c, item=item: (copy(item, s).start(), c)[1], 0)
        for item in range(count):
            mine = my_rank(items[item][1])
            targets[item][mine] = row(item, mine)[...]
        for item in range(count):
            axes, size = items[item][1], sizes[item]

            def finish(step, carry, item=item, axes=axes, size=size):
                mine = my_rank(axes)
                rank = lax.rem(mine + size - step, size)
                pltpu.make_async_remote_copy(
                    src_ref=row(item, mine),
                    dst_ref=targets[item].at[rank],
                    send_sem=send_sems[item].at[step],
                    recv_sem=recv_sems[item].at[step],
                    device_id=place(axes, rank),
                    device_id_type=MESH,
                ).wait()
                return carry

            lax.fori_loop(1, size, finish, 0)

    return pl.pallas_call(
        kernel,
        out_shape=outs,
        in_specs=[vmem] * count,
        out_specs=[vmem] * count,
        scratch_shapes=[pltpu.SemaphoreType.DMA((size,)) for size in sizes] * 2,
        compiler_params=pltpu.CompilerParams(collective_id=collective_id, has_side_effects=True),
    )(*[array for array, _, _ in items])


def split(table):
    high = jnp.asarray(table, f32).astype(bf16)
    return high, (jnp.asarray(table, f32) - high.astype(f32)).astype(bf16)


def fourier_tables(height, depth, sign):
    def parts(length):
        counter = np.arange(length)
        angles = (counter[:, None] * counter[None, :] % length) * (2.0 * np.pi / length)
        return np.cos(angles) / np.sqrt(length), sign * np.sin(angles) / np.sqrt(length)

    depth_cos, depth_sin = parts(depth)
    height_cos, height_sin = parts(height)
    along = np.block([[depth_cos, depth_sin], [-depth_sin, depth_cos]])
    down = np.concatenate([height_cos, height_sin], axis=0)
    return split(along) + split(down)


def dot(left, right):
    return jnp.dot(left, right, preferred_element_type=f32)


def halves(values):
    high = values.astype(bf16)
    return high, (values - high.astype(f32)).astype(bf16)


def spectrum(values, tables):
    along_high, along_low, down_high, down_low = tables
    height, depth = values.shape[0], values.shape[1] // 2
    high, low = halves(values)
    high, low = halves(
        dot(high, along_high[...]) + (dot(low, along_high[...]) + dot(high, along_low[...]))
    )
    both_parts = dot(down_high[...], high) + (dot(down_high[...], low) + dot(down_low[...], high))
    upper, lower = both_parts[:height], both_parts[height:]
    return jnp.concatenate(
        [upper[:, :depth] - lower[:, depth:], lower[:, :depth] + upper[:, depth:]], axis=1
    )


def coil_sum(real, imag, maps, kspace, mask, tables):
    total_real, total_imag = None, None
    for coil in range(maps.shape[0]):
        map_real, map_imag = maps[coil, 0, 0], maps[coil, 1, 0]
        image = jnp.concatenate(
            [map_real * real - map_imag * imag, map_real * imag + map_imag * real], axis=1
        )
        freq = spectrum(image, tables[:4])
        if kspace is not None:
            freq = freq - jnp.concatenate([kspace[coil, 0, 0], kspace[coil, 1, 0]], axis=1)
        back = spectrum(mask * freq, tables[4:])
        depth = real.shape[1]
        back_real, back_imag = back[:, :depth], back[:, depth:]
        part_real = map_real * back_real + map_imag * back_imag
        part_imag = map_real * back_imag - map_imag * back_real
        total_real = part_real if total_real is None else total_real + part_real
        total_imag = part_imag if total_imag is None else total_imag + part_imag
    return total_real, total_imag


def column(gathered, channel):
    return jnp.concatenate(
        [gathered[block, channel].astype(f32) for block in range(gathered.shape[0])], axis=0
    )


def data_kernel(place, gathered, maps, kspace, mask, *rest):
    tables, (parts_out, fields_out, padded) = rest[:8], rest[8:]
    height, depth = mask.shape
    pieces, window = parts_out.shape[0], parts_out.shape[2]
    own = window - 2 * reach
    weight = mask[...].astype(f32)
    weight = jnp.concatenate([weight, weight], axis=1)
    real, imag = column(gathered, 0), column(gathered, 1)
    padded[:, 0:8] = jnp.zeros((padded.shape[0], 8, depth), f32)
    padded[:, height + reach : height + reach + 8] = jnp.zeros((padded.shape[0], 8, depth), f32)
    for channel in range(fields_out.shape[1]):
        padded[channel, reach : reach + height] = column(gathered, channel)
    slabs = fields_out.shape[0]
    first = place[0] * (slabs * own)
    for piece in range(slabs):
        start = first + piece * own
        fields_out[piece] = padded[:, pl.ds(start, window), :].astype(bf16)
    total_real, total_imag = coil_sum(real, imag, maps, kspace, weight, tables)
    padded[0, reach : reach + height] = total_real
    padded[1, reach : reach + height] = total_imag
    for piece in range(pieces):
        parts_out[piece] = padded[0:2, piece * own : piece * own + window, :].astype(bf16)


def normal_kernel(gathered, pulled, maps, mask, *rest):
    tables, out = rest[:8], rest[8]
    weight = mask[...].astype(f32)
    weight = jnp.concatenate([weight, weight], axis=1)
    blocks, rows = out.shape[0], out.shape[2]
    for field in range(2):
        real = column(gathered, 2 + 2 * field) + column(pulled, 2 * field)
        imag = column(gathered, 3 + 2 * field) + column(pulled, 2 * field + 1)
        sums = coil_sum(real, imag, maps, None, weight, tables)
        for part in range(2):
            for block in range(blocks):
                out[block, 2 * field + part] = sums[part][block * rows : (block + 1) * rows].astype(bf16)


def banded(kernel, slices, form):
    outs, ins = kernel.shape[:2]
    order = {"in": (2, 0, 3, 4, 1), "mid": (3, 2, 0, 4, 1), "out": (3, 4, 2, 0, 1)}[form]
    taps, units = {"in": (1, 9), "mid": (3, 3), "out": (9, 1)}[form]
    small = jnp.transpose(kernel, order).reshape(taps * 3 * outs, units * ins)
    spread = np.kron(np.eye(units), np.tile(np.eye(ins), (1, slices)))
    wide = dot(small, jnp.asarray(spread, bf16)).reshape(taps, 1, 3, outs, -1)
    lane_slice = np.tile(np.repeat(np.arange(slices), ins), units)
    inside = (
        lane_slice[None, None, :]
        == (np.arange(slices)[:, None, None] + np.arange(3)[None, :, None] - 1)
    )
    chosen = wide * jnp.asarray(inside, f32)[None, :, :, None, :]
    return chosen.sum(2).astype(bf16).reshape(taps, slices * outs, -1)


def transposed(kernel):
    return jnp.swapaxes(jnp.flip(kernel, (2, 3, 4)), 0, 1)


def shifted(values, tap, depth):
    if tap == 1:
        return values
    lane = lax.broadcasted_iota(jnp.int32, (values.shape[0], depth), 1)
    edge, turn = (0, 1) if tap == 0 else (depth - 1, depth - 1)
    pieces = []
    for start in range(0, values.shape[1], depth):
        turned = pltpu.roll(values[:, start : start + depth], turn, 1)
        pieces.append(jnp.where(lane == edge, 0.0, turned))
    return jnp.concatenate(pieces, axis=1)


def conv_in(values, weights, depth):
    width = values.shape[1] - 2 * depth
    turned = [shifted(values, tap, depth) for tap in range(3)]
    stacked = jnp.concatenate(
        [turned[dz][:, dy * depth : dy * depth + width] for dy in range(3) for dz in range(3)],
        axis=0,
    )
    return dot(weights[0], stacked.astype(bf16))


def conv_mid(values, weights, depth):
    width = values.shape[1] - 2 * depth
    stacked = jnp.concatenate(
        [shifted(values, tap, depth).astype(bf16) for tap in range(3)], axis=0
    )
    total = None
    for dy in range(3):
        term = dot(weights[dy], stacked[:, dy * depth : dy * depth + width])
        total = term if total is None else total + term
    return total


def conv_out(values, weights, depth):
    width = values.shape[1] - 2 * depth
    taps, rows, inner = weights.shape
    products = dot(weights[...].reshape(taps * rows, inner), values.astype(bf16))
    total = None
    for dz in range(3):
        summed = None
        for dy in range(3):
            at = (dy * 3 + dz) * rows
            term = products[at : at + rows, dy * depth : dy * depth + width]
            summed = term if summed is None else summed + term
        term = shifted(summed, dz, depth)
        total = term if total is None else total + term
    return total


def conv_kernel(place, parts, fields, first, second, last, first_t, second_t, last_t,
                pulled_out, delta_out, work, rows_work):
    slices, channels, window, depth = fields.shape
    coils = parts.shape[0] // slices
    own = window - 2 * reach
    height = coils * slices * own
    row_base = place[0] * own - reach

    def load(values):
        work[...] = values.reshape(work.shape)
        return jnp.concatenate([work[:, row, :] for row in range(window)], axis=1)

    def cut(values, before, after):
        return values[:, before * depth : values.shape[1] - after * depth]

    def inside(values, offset):
        pieces = []
        for row in range(values.shape[1] // depth):
            at = row_base + offset + row
            keep = jnp.where((at >= 0) & (at < height), 1.0, 0.0).astype(f32)
            pieces.append(values[:, row * depth : (row + 1) * depth] * keep)
        return jnp.concatenate(pieces, axis=1)

    def store(values):
        for row in range(own):
            rows_work[:, row, :] = values[:, row * depth : (row + 1) * depth]
        return rows_work[...].reshape(slices, 2, own, depth)

    summed = parts[0:slices].astype(f32)
    for coil in range(1, coils):
        summed = summed + parts[coil * slices : (coil + 1) * slices].astype(f32)
    moved = load(-step_size * summed)
    relaxed = load(fields[:, 0:2].astype(f32)) + moved
    pre1 = conv_in(relaxed.astype(bf16).astype(f32), first, depth)
    sig1 = jax.nn.sigmoid(pre1)
    act1 = inside((pre1 * sig1), 1)
    slope1 = sig1 * (1.0 + pre1 * (1.0 - sig1))
    pre2 = conv_mid(act1, second, depth)
    sig2 = jax.nn.sigmoid(pre2)
    slope2 = inside(sig2 * (1.0 + pre2 * (1.0 - sig2)), 2)
    act2 = inside(cut(pre2 * sig2, 1, 1), 3)
    delta = conv_out(act2, last, depth) + cut(moved, reach, reach)
    delta_out[...] = store(delta)
    slope1 = inside(cut(slope1, 2, 2), 3)
    for field in range(2):
        probe = cut(load(fields[:, 2 + 2 * field : 4 + 2 * field].astype(f32)), 1, 1)
        grad2 = conv_in(probe, last_t, depth) * slope2
        grad1 = conv_mid(grad2, second_t, depth) * slope1
        grad0 = conv_out(grad1, first_t, depth)
        pulled_out[:, 2 * field : 2 * field + 2] = store(grad0).astype(bf16)


def on_device(coil_maps, kspace, sample_mask, iterate, probe_bits, loss_gradient, adjoint,
              kernel_first, kernel_second, kernel_last):
    height, depth = sample_mask.shape
    coils, slabs = lax.axis_size("coil"), lax.axis_size("slab")
    pieces = coils * slabs
    own = height // pieces
    window = own + 2 * reach
    rows = iterate.shape[2]
    my_coil, my_slab = lax.axis_index("coil"), lax.axis_index("slab")
    rank = my_coil * slabs + my_slab
    smem = pl.BlockSpec(memory_space=pltpu.SMEM)
    tables = fourier_tables(height, depth, -1.0) + fourier_tables(height, depth, 1.0)

    sign_field = (2 * probe_bits - 1).astype(f32)
    own_fields = jnp.concatenate([iterate, sign_field, adjoint], axis=0)[:, 0].astype(bf16)
    (gathered,) = exchange([(own_fields, ("coil",), "all")], 0)
    parts, fields = pl.pallas_call(
        data_kernel,
        out_shape=[
            jax.ShapeDtypeStruct((pieces, 2, window, depth), bf16),
            jax.ShapeDtypeStruct((slabs, 6, window, depth), bf16),
        ],
        in_specs=[smem] + [vmem] * 12,
        out_specs=[vmem] * 2,
        scratch_shapes=[pltpu.VMEM((6, height + 2 * reach + 8, depth), f32)],
    )(my_coil.reshape(1), gathered, coil_maps, kspace, sample_mask, *tables)
    parts, fields = exchange([(parts, both, "row"), (fields, ("slab",), "row")], 1)

    forward = [
        banded(kernel, slabs, form)
        for kernel, form in ((kernel_first, "in"), (kernel_second, "mid"), (kernel_last, "out"))
    ]
    backward = [
        banded(transposed(kernel), slabs, form)
        for kernel, form in ((kernel_first, "out"), (kernel_second, "mid"), (kernel_last, "in"))
    ]
    pulled, delta = pl.pallas_call(
        conv_kernel,
        out_shape=[
            jax.ShapeDtypeStruct((slabs, 4, own, depth), bf16),
            jax.ShapeDtypeStruct((slabs, 2, own, depth), f32),
        ],
        in_specs=[smem] + [vmem] * 8,
        out_specs=[vmem] * 2,
        scratch_shapes=[
            pltpu.VMEM((2 * slabs, window, depth), f32),
            pltpu.VMEM((2 * slabs, own, depth), f32),
        ],
    )(rank.reshape(1), parts, fields, *forward, *backward)
    pulled, delta = exchange([(pulled, both, "slab"), (delta, ("slab",), "row")], 2)
    new_iterate = iterate + jnp.swapaxes(delta, 0, 1).reshape(2, 1, rows, depth)

    sums = pl.pallas_call(
        normal_kernel,
        out_shape=jax.ShapeDtypeStruct((coils, 4, rows, depth), bf16),
        in_specs=[vmem] * 12,
        out_specs=vmem,
    )(gathered, pulled, coil_maps, sample_mask, *tables)
    (sums,) = exchange([(sums, ("coil",), "row")], 3)
    mine = lax.dynamic_slice_in_dim(pulled, my_coil * slabs, slabs, 0).astype(f32)
    mine = jnp.swapaxes(mine, 0, 1).reshape(4, rows, depth)
    step = mine - step_size * sums.astype(f32).sum(0)
    probe_pullback = sign_field + step[0:2, None]
    adjoint_next = loss_gradient + (adjoint + step[2:4, None])
    return new_iterate, probe_pullback, adjoint_next


def solution(mesh):
    split_coils = P("coil", None, "slab", None, None)
    image = P(None, "slab", "coil", None)
    return jax.shard_map(
        on_device,
        mesh=mesh,
        in_specs=(split_coils, split_coils, P(), image, image, image, image, P(), P(), P()),
        out_specs=(image, image, image),
        check_vma=False,
    )
```

```python
import math

import jax
import jax.numpy as jnp
import numpy as np
from jax import lax
from jax.experimental import pallas as pl
from jax.experimental.pallas import tpu as pltpu
from jax.sharding import PartitionSpec as P

step_size = 0.8
reach = 4
both = ("coil", "slab")
f32 = jnp.float32
bf16 = jnp.bfloat16
vmem = pl.BlockSpec(memory_space=pltpu.VMEM)
MESH = pl.DeviceIdType.MESH


class Channel:
    def __init__(self, axes, how, source, target, send_sem, recv_sem):
        self.axes, self.how, self.source, self.target = axes, how, source, target
        self.send_sem, self.recv_sem = send_sem, recv_sem
        self.size = math.prod(lax.axis_size(axis) for axis in axes)
        self.mine = rank_of(axes)

    def row(self, rank):
        if self.how == "all":
            return self.source
        if self.how == "slab":
            return self.source.at[place_of(self.axes, rank)[1]]
        return self.source.at[rank]

    def copy(self, source_rank, target_row, device_rank, step):
        return pltpu.make_async_remote_copy(
            src_ref=self.row(source_rank),
            dst_ref=self.target.at[target_row],
            send_sem=self.send_sem.at[step],
            recv_sem=self.recv_sem.at[step],
            device_id=place_of(self.axes, device_rank),
            device_id_type=MESH,
        )

    def start(self):
        def send(step, carry):
            rank = lax.rem(self.mine + step, self.size)
            self.copy(rank, self.mine, rank, step).start()
            return carry

        lax.fori_loop(1, self.size, send, 0)
        self.target[self.mine] = self.row(self.mine)[...]

    def finish(self):
        def wait(step, carry):
            rank = lax.rem(self.mine + self.size - step, self.size)
            self.copy(self.mine, rank, rank, step).wait()
            return carry

        lax.fori_loop(1, self.size, wait, 0)


def rank_of(axes):
    if axes == both:
        return lax.axis_index("coil") * lax.axis_size("slab") + lax.axis_index("slab")
    return lax.axis_index(axes[0])


def place_of(axes, rank):
    slabs = lax.axis_size("slab")
    if axes == both:
        return lax.div(rank, slabs), lax.rem(rank, slabs)
    return (rank, lax.axis_index("slab")) if axes == ("coil",) else (lax.axis_index("coil"), rank)


def greet_all():
    barrier = pltpu.get_barrier_semaphore()
    size = lax.axis_size("coil") * lax.axis_size("slab")

    def greet(step, carry):
        rank = lax.rem(rank_of(both) + step, size)
        pl.semaphore_signal(barrier, inc=1, device_id=place_of(both, rank), device_id_type=MESH)
        return carry

    lax.fori_loop(1, size, greet, 0)
    return barrier, size - 1


def split(table):
    high = jnp.asarray(table, f32).astype(bf16)
    return high, (jnp.asarray(table, f32) - high.astype(f32)).astype(bf16)


def fourier_tables(height, depth, sign):
    def parts(length):
        counter = np.arange(length)
        angles = (counter[:, None] * counter[None, :] % length) * (2.0 * np.pi / length)
        return np.cos(angles) / np.sqrt(length), sign * np.sin(angles) / np.sqrt(length)

    depth_cos, depth_sin = parts(depth)
    height_cos, height_sin = parts(height)
    along = np.block([[depth_cos, depth_sin], [-depth_sin, depth_cos]])
    down = np.concatenate([height_cos, height_sin], axis=0)
    return split(along) + split(down)


def dot(left, right):
    return jnp.dot(left, right, preferred_element_type=f32)


def halves(values):
    high = values.astype(bf16)
    return high, (values - high.astype(f32)).astype(bf16)


def spectrum(values, tables):
    along_high, along_low, down_high, down_low = tables
    height, depth = values.shape[0], values.shape[1] // 2
    high, low = halves(values)
    high, low = halves(
        dot(high, along_high[...]) + (dot(low, along_high[...]) + dot(high, along_low[...]))
    )
    both_parts = dot(down_high[...], high) + (dot(down_high[...], low) + dot(down_low[...], high))
    upper, lower = both_parts[:height], both_parts[height:]
    return jnp.concatenate(
        [upper[:, :depth] - lower[:, depth:], lower[:, :depth] + upper[:, depth:]], axis=1
    )


def coil_term(real, imag, coil, maps, kspace, mask, tables):
    depth = real.shape[1]
    map_real, map_imag = maps[coil, 0, 0], maps[coil, 1, 0]
    image = jnp.concatenate(
        [map_real * real - map_imag * imag, map_real * imag + map_imag * real], axis=1
    )
    freq = spectrum(image, tables[:4])
    if kspace is not None:
        freq = freq - jnp.concatenate([kspace[coil, 0, 0], kspace[coil, 1, 0]], axis=1)
    back = spectrum(mask * freq, tables[4:])
    back_real, back_imag = back[:, :depth], back[:, depth:]
    return (
        map_real * back_real + map_imag * back_imag,
        map_real * back_imag - map_imag * back_real,
    )


def column(gathered, channel):
    return jnp.concatenate(
        [gathered[block, channel].astype(f32) for block in range(gathered.shape[0])], axis=0
    )


def banded(kernel, slices, form):
    outs, ins = kernel.shape[:2]
    order = {"in": (2, 0, 3, 4, 1), "mid": (3, 2, 0, 4, 1), "out": (3, 4, 2, 0, 1)}[form]
    taps, units = {"in": (1, 9), "mid": (3, 3), "out": (9, 1)}[form]
    small = jnp.transpose(kernel, order).reshape(taps * 3 * outs, units * ins)
    spread = np.kron(np.eye(units), np.tile(np.eye(ins), (1, slices)))
    wide = dot(small, jnp.asarray(spread, bf16)).reshape(taps, 1, 3, outs, -1)
    lane_slice = np.tile(np.repeat(np.arange(slices), ins), units)
    inside = (
        lane_slice[None, None, :]
        == (np.arange(slices)[:, None, None] + np.arange(3)[None, :, None] - 1)
    )
    chosen = wide * jnp.asarray(inside, f32)[None, :, :, None, :]
    return chosen.sum(2).astype(bf16).reshape(taps, slices * outs, -1)


def transposed(kernel):
    return jnp.swapaxes(jnp.flip(kernel, (2, 3, 4)), 0, 1)


def shifted(values, tap, depth):
    if tap == 1:
        return values
    lane = lax.broadcasted_iota(jnp.int32, (values.shape[0], depth), 1)
    edge, turn = (0, 1) if tap == 0 else (depth - 1, depth - 1)
    pieces = []
    for start in range(0, values.shape[1], depth):
        turned = pltpu.roll(values[:, start : start + depth], turn, 1)
        pieces.append(jnp.where(lane == edge, 0.0, turned))
    return jnp.concatenate(pieces, axis=1)


def conv_in(values, weights, depth):
    width = values.shape[1] - 2 * depth
    turned = [shifted(values, tap, depth) for tap in range(3)]
    stacked = jnp.concatenate(
        [turned[dz][:, dy * depth : dy * depth + width] for dy in range(3) for dz in range(3)],
        axis=0,
    )
    return dot(weights[0], stacked.astype(bf16))


def conv_mid(values, weights, depth):
    width = values.shape[1] - 2 * depth
    stacked = jnp.concatenate(
        [shifted(values, tap, depth).astype(bf16) for tap in range(3)], axis=0
    )
    total = None
    for dy in range(3):
        term = dot(weights[dy], stacked[:, dy * depth : dy * depth + width])
        total = term if total is None else total + term
    return total


def conv_out(values, weights, depth):
    width = values.shape[1] - 2 * depth
    taps, rows, inner = weights.shape
    products = dot(weights[...].reshape(taps * rows, inner), values.astype(bf16))
    total = None
    for dz in range(3):
        summed = None
        for dy in range(3):
            at = (dy * 3 + dz) * rows
            term = products[at : at + rows, dy * depth : dy * depth + width]
            summed = term if summed is None else summed + term
        term = shifted(summed, dz, depth)
        total = term if total is None else total + term
    return total


def step_kernel(maps, kspace, mask, iterate, probe_bits, loss_gradient, adjoint, *rest):
    tables, weights, rest = rest[:8], rest[8:14], rest[14:]
    first, second, last, first_t, second_t, last_t = weights
    new_out, probe_out, adjoint_out = rest[:3]
    (padded, work, rows_work, own_iterate, own_fields, all_iterate, all_fields, parts_send, parts,
     fields_send, fields, delta_send, delta, pulled_send, pulled, sums_send, sums) = rest[3:20]
    sems = rest[20:]
    channels = []
    for index, (axes, how, source, target) in enumerate((
        (("coil",), "all", own_iterate, all_iterate),
        (("coil",), "all", own_fields, all_fields),
        (("slab",), "row", fields_send, fields),
        (both, "row", parts_send, parts),
        (("slab",), "row", delta_send, delta),
        (both, "slab", pulled_send.at[0], pulled.at[0]),
        (both, "slab", pulled_send.at[1], pulled.at[1]),
        (("coil",), "row", sums_send.at[0], sums.at[0]),
        (("coil",), "row", sums_send.at[1], sums.at[1]),
    )):
        channels.append(Channel(axes, how, source, target, sems[2 * index], sems[2 * index + 1]))
    (iterate_way, field_way, window_way, part_way, delta_way, *later) = channels
    pulled_ways, sum_ways = later[:2], later[2:]

    height, depth = mask.shape
    coils, rows = all_iterate.shape[0], all_iterate.shape[2]
    pieces, _, window, _ = parts.shape
    slices = fields.shape[0]
    own = window - 2 * reach
    my_coil = lax.axis_index("coil")
    row_base = rank_of(both) * own - reach

    barrier, arrivals = greet_all()
    sign = (2 * probe_bits[...] - 1).astype(f32)
    own_iterate[...] = iterate[:, 0].astype(bf16)
    own_fields[0:2] = sign[:, 0].astype(bf16)
    own_fields[2:4] = adjoint[:, 0].astype(bf16)
    edge = jnp.zeros((6, 8, depth), f32)
    padded[:, 0:8] = edge
    padded[:, height + reach : height + reach + 8] = edge
    weight = mask[...].astype(f32)
    weight = jnp.concatenate([weight, weight], axis=1)
    pl.semaphore_wait(barrier, arrivals)
    iterate_way.start()
    field_way.start()
    iterate_way.finish()

    real, imag = column(all_iterate, 0), column(all_iterate, 1)
    total_real, total_imag = coil_term(real, imag, 0, maps, kspace, weight, tables)
    field_way.finish()
    padded[0, reach : reach + height] = real
    padded[1, reach : reach + height] = imag
    for channel in range(4):
        padded[2 + channel, reach : reach + height] = column(all_fields, channel)
    for piece in range(slices):
        start = my_coil * (slices * own) + piece * own
        fields_send[piece] = padded[:, pl.ds(start, window), :].astype(bf16)
    window_way.start()
    for coil in range(1, maps.shape[0]):
        more_real, more_imag = coil_term(real, imag, coil, maps, kspace, weight, tables)
        total_real, total_imag = total_real + more_real, total_imag + more_imag
    padded[0, reach : reach + height] = total_real
    padded[1, reach : reach + height] = total_imag
    for piece in range(pieces):
        parts_send[piece] = padded[0:2, piece * own : piece * own + window, :].astype(bf16)
    part_way.start()

    def load(values):
        work[...] = values.reshape(work.shape)
        return jnp.concatenate([work[:, row, :] for row in range(window)], axis=1)

    def cut(values, before, after):
        return values[:, before * depth : values.shape[1] - after * depth]

    def inside(values, offset):
        blocks = []
        for row in range(values.shape[1] // depth):
            at = row_base + offset + row
            keep = jnp.where((at >= 0) & (at < height), 1.0, 0.0).astype(f32)
            blocks.append(values[:, row * depth : (row + 1) * depth] * keep)
        return jnp.concatenate(blocks, axis=1)

    def store(values):
        for row in range(own):
            rows_work[:, row, :] = values[:, row * depth : (row + 1) * depth]
        return rows_work[...].reshape(slices, 2, own, depth)

    window_way.finish()
    started = load(fields[:, 0:2].astype(f32))
    grads = []
    for field in range(2):
        probe = cut(load(fields[:, 2 + 2 * field : 4 + 2 * field].astype(f32)), 1, 1)
        grads.append(conv_in(probe, last_t, depth))
    part_way.finish()
    summed = parts[0:slices].astype(f32)
    for coil in range(1, coils):
        summed = summed + parts[coil * slices : (coil + 1) * slices].astype(f32)
    moved = load(-step_size * summed)
    relaxed = started + moved
    pre1 = conv_in(relaxed.astype(bf16).astype(f32), first, depth)
    sig1 = jax.nn.sigmoid(pre1)
    act1 = inside(pre1 * sig1, 1)
    slope1 = inside(cut(sig1 * (1.0 + pre1 * (1.0 - sig1)), 2, 2), 3)
    pre2 = conv_mid(act1, second, depth)
    sig2 = jax.nn.sigmoid(pre2)
    slope2 = inside(sig2 * (1.0 + pre2 * (1.0 - sig2)), 2)
    for field in range(2):
        grad1 = conv_mid(grads[field] * slope2, second_t, depth) * slope1
        pulled_send[field] = store(conv_out(grad1, first_t, depth)).astype(bf16)
        pulled_ways[field].start()
    act2 = inside(cut(pre2 * sig2, 1, 1), 3)
    delta_send[...] = store(conv_out(act2, last, depth) + cut(moved, reach, reach))
    delta_way.start()

    for field in range(2):
        pulled_ways[field].finish()
        real = column(all_fields, 2 * field) + column(pulled.at[field], 0)
        imag = column(all_fields, 2 * field + 1) + column(pulled.at[field], 1)
        total = None
        for coil in range(maps.shape[0]):
            term = coil_term(real, imag, coil, maps, None, weight, tables)
            total = term if total is None else (total[0] + term[0], total[1] + term[1])
        for part in range(2):
            for block in range(coils):
                at = block * rows
                sums_send[field, block, part] = total[part][at : at + rows].astype(bf16)
        sum_ways[field].start()

    delta_way.finish()
    for part in range(2):
        for piece in range(slices):
            at = piece * own
            new_out[part, 0, at : at + own] = iterate[part, 0, at : at + own] + delta[piece, part]
    starts = (sign, loss_gradient[...] + adjoint[...])
    for field, out in ((0, probe_out), (1, adjoint_out)):
        sum_ways[field].finish()
        for part in range(2):
            added = sums[field, 0, part].astype(f32)
            for block in range(1, coils):
                added = added + sums[field, block, part].astype(f32)
            mine = jnp.concatenate(
                [
                    pulled[field, my_coil * slices + piece, part].astype(f32)
                    for piece in range(slices)
                ],
                axis=0,
            )
            out[part, 0] = starts[field][part, 0] + (mine - step_size * added)


def on_device(coil_maps, kspace, sample_mask, iterate, probe_bits, loss_gradient, adjoint,
              kernel_first, kernel_second, kernel_last):
    height, depth = sample_mask.shape
    coils, slabs = lax.axis_size("coil"), lax.axis_size("slab")
    pieces = coils * slabs
    own = height // pieces
    window = own + 2 * reach
    rows = iterate.shape[2]
    tables = fourier_tables(height, depth, -1.0) + fourier_tables(height, depth, 1.0)
    forward = [
        banded(kernel, slabs, form)
        for kernel, form in ((kernel_first, "in"), (kernel_second, "mid"), (kernel_last, "out"))
    ]
    backward = [
        banded(transposed(kernel), slabs, form)
        for kernel, form in ((kernel_first, "out"), (kernel_second, "mid"), (kernel_last, "in"))
    ]
    buffers = [
        ((6, height + 2 * reach + 8, depth), f32),
        ((2 * slabs, window, depth), f32),
        ((2 * slabs, own, depth), f32),
        ((2, rows, depth), bf16),
        ((4, rows, depth), bf16),
        ((coils, 2, rows, depth), bf16),
        ((coils, 4, rows, depth), bf16),
        ((pieces, 2, window, depth), bf16),
        ((pieces, 2, window, depth), bf16),
        ((slabs, 6, window, depth), bf16),
        ((slabs, 6, window, depth), bf16),
        ((slabs, 2, own, depth), f32),
        ((slabs, 2, own, depth), f32),
        ((2, slabs, 2, own, depth), bf16),
        ((2, pieces, 2, own, depth), bf16),
        ((2, coils, 2, rows, depth), bf16),
        ((2, coils, 2, rows, depth), bf16),
    ]
    ways = (coils, coils, slabs, pieces, slabs, pieces, pieces, coils, coils)
    return pl.pallas_call(
        step_kernel,
        out_shape=[jax.ShapeDtypeStruct(iterate.shape, f32)] * 3,
        in_specs=[vmem] * 21,
        out_specs=[vmem] * 3,
        scratch_shapes=[pltpu.VMEM(shape, kind) for shape, kind in buffers]
        + [pltpu.SemaphoreType.DMA((size,)) for size in ways for _ in range(2)],
        compiler_params=pltpu.CompilerParams(collective_id=0, has_side_effects=True),
    )(coil_maps, kspace, sample_mask, iterate, probe_bits, loss_gradient, adjoint,
      *tables, *forward, *backward)


def solution(mesh):
    split_coils = P("coil", None, "slab", None, None)
    image = P(None, "slab", "coil", None)
    return jax.shard_map(
        on_device,
        mesh=mesh,
        in_specs=(split_coils, split_coils, P(), image, image, image, image, P(), P(), P()),
        out_specs=(image, image, image),
        check_vma=False,
    )
```

```python
import math

import jax
import jax.numpy as jnp
import numpy as np
from jax import lax
from jax.experimental import pallas as pl
from jax.experimental.pallas import tpu as pltpu
from jax.sharding import PartitionSpec as P

step_size = 0.8
reach = 4
both = ("coil", "slab")
f32 = jnp.float32
bf16 = jnp.bfloat16
vmem = pl.BlockSpec(memory_space=pltpu.VMEM)
MESH = pl.DeviceIdType.MESH


class Channel:
    def __init__(self, axes, how, source, target, send_sem, recv_sem):
        self.axes, self.how, self.source, self.target = axes, how, source, target
        self.send_sem, self.recv_sem = send_sem, recv_sem
        self.size = math.prod(lax.axis_size(axis) for axis in axes)
        self.mine = rank_of(axes)

    def row(self, rank):
        if self.how == "all":
            return self.source
        if self.how == "slab":
            return self.source.at[place_of(self.axes, rank)[1]]
        return self.source.at[rank]

    def copy(self, source_rank, target_row, device_rank, step):
        return pltpu.make_async_remote_copy(
            src_ref=self.row(source_rank),
            dst_ref=self.target.at[target_row],
            send_sem=self.send_sem.at[step],
            recv_sem=self.recv_sem.at[step],
            device_id=place_of(self.axes, device_rank),
            device_id_type=MESH,
        )

    def start(self):
        def send(step, carry):
            rank = lax.rem(self.mine + step, self.size)
            self.copy(rank, self.mine, rank, step).start()
            return carry

        lax.fori_loop(1, self.size, send, 0)
        self.target[self.mine] = self.row(self.mine)[...]

    def finish(self):
        def wait(step, carry):
            rank = lax.rem(self.mine + self.size - step, self.size)
            self.copy(self.mine, rank, rank, step).wait()
            return carry

        lax.fori_loop(1, self.size, wait, 0)


def rank_of(axes):
    if axes == both:
        return lax.axis_index("coil") * lax.axis_size("slab") + lax.axis_index("slab")
    return lax.axis_index(axes[0])


def place_of(axes, rank):
    slabs = lax.axis_size("slab")
    if axes == both:
        return lax.div(rank, slabs), lax.rem(rank, slabs)
    return (rank, lax.axis_index("slab")) if axes == ("coil",) else (lax.axis_index("coil"), rank)


def greet_all():
    barrier = pltpu.get_barrier_semaphore()
    size = lax.axis_size("coil") * lax.axis_size("slab")

    def greet(step, carry):
        rank = lax.rem(rank_of(both) + step, size)
        pl.semaphore_signal(barrier, inc=1, device_id=place_of(both, rank), device_id_type=MESH)
        return carry

    lax.fori_loop(1, size, greet, 0)
    return barrier, size - 1


def split(table):
    high = jnp.asarray(table, f32).astype(bf16)
    return high, (jnp.asarray(table, f32) - high.astype(f32)).astype(bf16)


def fourier_tables(height, depth, sign):
    def parts(length):
        counter = np.arange(length)
        angles = (counter[:, None] * counter[None, :] % length) * (2.0 * np.pi / length)
        return np.cos(angles) / np.sqrt(length), sign * np.sin(angles) / np.sqrt(length)

    depth_cos, depth_sin = parts(depth)
    height_cos, height_sin = parts(height)
    along = np.block([[depth_cos, depth_sin], [-depth_sin, depth_cos]])
    down = np.concatenate([height_cos, height_sin], axis=0)
    return split(along) + split(down)


def dot(left, right):
    return jnp.dot(left, right, preferred_element_type=f32)


def halves(values):
    high = values.astype(bf16)
    return high, (values - high.astype(f32)).astype(bf16)


def spectrum(values, tables):
    along_high, along_low, down_high, down_low = tables
    height, depth = values.shape[0], values.shape[1] // 2
    high, low = halves(values)
    high, low = halves(
        dot(high, along_high[...]) + (dot(low, along_high[...]) + dot(high, along_low[...]))
    )
    both_parts = dot(down_high[...], high) + (dot(down_high[...], low) + dot(down_low[...], high))
    upper, lower = both_parts[:height], both_parts[height:]
    return jnp.concatenate(
        [upper[:, :depth] - lower[:, depth:], lower[:, :depth] + upper[:, depth:]], axis=1
    )


def coil_term(real, imag, coil, maps, kspace, mask, tables):
    depth = real.shape[1]
    map_real, map_imag = maps[coil, 0, 0], maps[coil, 1, 0]
    image = jnp.concatenate(
        [map_real * real - map_imag * imag, map_real * imag + map_imag * real], axis=1
    )
    freq = spectrum(image, tables[:4])
    if kspace is not None:
        freq = freq - jnp.concatenate([kspace[coil, 0, 0], kspace[coil, 1, 0]], axis=1)
    back = spectrum(mask * freq, tables[4:])
    back_real, back_imag = back[:, :depth], back[:, depth:]
    return (
        map_real * back_real + map_imag * back_imag,
        map_real * back_imag - map_imag * back_real,
    )


def column(gathered, channel):
    return jnp.concatenate(
        [gathered[block, channel].astype(f32) for block in range(gathered.shape[0])], axis=0
    )


forms = {"in": ((2, 0, 3, 4, 1), 1, 9), "mid": ((3, 2, 0, 4, 1), 3, 3), "out": ((3, 4, 2, 0, 1), 9, 1)}


def small_kernel(kernel, form):
    order, taps, units = forms[form]
    outs, ins = kernel.shape[:2]
    return jnp.transpose(kernel, order).reshape(taps * 3 * outs, units * ins)


def band_constants(kernel, slices, form):
    _, taps, units = forms[form]
    outs, ins = kernel.shape[:2]
    spread = jnp.asarray(np.kron(np.eye(units), np.tile(np.eye(ins), (1, slices))), bf16)
    lanes = np.tile(np.repeat(np.arange(slices), ins), units)
    if form != "out":
        return spread, jnp.asarray(lanes[None, :], f32)
    row_slices = np.repeat(np.arange(slices), outs)
    bands = np.stack([lanes[None, :] == row_slices[:, None] + dx - 1 for dx in range(3)])
    repeat = np.stack(
        [
            np.kron(np.eye(taps), np.tile(np.eye(3 * outs)[dx * outs : (dx + 1) * outs], (slices, 1)))
            for dx in range(3)
        ]
    )
    return spread, jnp.asarray(bands, f32), jnp.asarray(repeat, bf16)


def build_rows(small, spread, lanes, target):
    taps, inner = target.shape[:2]
    outs = small.shape[0] // (3 * taps)
    wide = dot(small[...], spread[...])
    lane_slice = lanes[...]
    for tap in range(taps):
        blocks = []
        for out_slice in range(inner // outs):
            block = None
            for dx in range(3):
                at = (tap * 3 + dx) * outs
                term = jnp.where(lane_slice == float(out_slice + dx - 1), wide[at : at + outs], 0.0)
                block = term if block is None else block + term
            blocks.append(block)
        target[tap] = jnp.concatenate(blocks, axis=0).astype(bf16)


def build_taps(small, spread, bands, repeat, target):
    wide = dot(small[...], spread[...]).astype(bf16)
    total = None
    for dx in range(3):
        term = dot(repeat[dx], wide).reshape(target.shape) * bands[dx][None]
        total = term if total is None else total + term
    target[...] = total.astype(bf16)


def transposed(kernel):
    return jnp.swapaxes(jnp.flip(kernel, (2, 3, 4)), 0, 1)


def shifted(values, tap, depth):
    if tap == 1:
        return values
    lane = lax.broadcasted_iota(jnp.int32, (values.shape[0], depth), 1)
    edge, turn = (0, 1) if tap == 0 else (depth - 1, depth - 1)
    pieces = []
    for start in range(0, values.shape[1], depth):
        turned = pltpu.roll(values[:, start : start + depth], turn, 1)
        pieces.append(jnp.where(lane == edge, 0.0, turned))
    return jnp.concatenate(pieces, axis=1)


def conv_in(values, weights, depth):
    width = values.shape[1] - 2 * depth
    turned = [shifted(values, tap, depth) for tap in range(3)]
    stacked = jnp.concatenate(
        [turned[dz][:, dy * depth : dy * depth + width] for dy in range(3) for dz in range(3)],
        axis=0,
    )
    return dot(weights[0], stacked.astype(bf16))


def conv_mid(values, weights, depth):
    width = values.shape[1] - 2 * depth
    stacked = jnp.concatenate(
        [shifted(values, tap, depth).astype(bf16) for tap in range(3)], axis=0
    )
    total = None
    for dy in range(3):
        term = dot(weights[dy], stacked[:, dy * depth : dy * depth + width])
        total = term if total is None else total + term
    return total


def conv_out(values, weights, depth):
    width = values.shape[1] - 2 * depth
    taps, rows, inner = weights.shape
    products = dot(weights[...].reshape(taps * rows, inner), values.astype(bf16))
    total = None
    for dz in range(3):
        summed = None
        for dy in range(3):
            at = (dy * 3 + dz) * rows
            term = products[at : at + rows, dy * depth : dy * depth + width]
            summed = term if summed is None else summed + term
        term = shifted(summed, dz, depth)
        total = term if total is None else total + term
    return total


def step_kernel(maps, kspace, mask, iterate, probe_bits, adjoint, *rest):
    tables, smalls, bands, rest = rest[:8], rest[8:14], rest[14:21], rest[21:]
    in_band, mid_band, out_band = bands[:2], bands[2:4], bands[4:]
    changes = rest[0]
    (padded, work, rows_work, own_iterate, own_fields, all_iterate, all_fields, parts_send, parts,
     fields_send, fields, delta_send, delta, pulled_send, pulled, sums_send, sums, *weights) = rest[1:24]
    first, second, last, first_t, second_t, last_t = weights
    sems = rest[24:]
    channels = []
    for index, (axes, how, source, target) in enumerate((
        (("coil",), "all", own_iterate, all_iterate),
        (("coil",), "all", own_fields, all_fields),
        (("slab",), "row", fields_send, fields),
        (both, "row", parts_send, parts),
        (("slab",), "row", delta_send, delta),
        (both, "slab", pulled_send.at[0], pulled.at[0]),
        (both, "slab", pulled_send.at[1], pulled.at[1]),
        (("coil",), "row", sums_send.at[0], sums.at[0]),
        (("coil",), "row", sums_send.at[1], sums.at[1]),
    )):
        channels.append(Channel(axes, how, source, target, sems[2 * index], sems[2 * index + 1]))
    (iterate_way, field_way, window_way, part_way, delta_way, *later) = channels
    pulled_ways, sum_ways = later[:2], later[2:]

    height, depth = mask.shape
    coils, rows = all_iterate.shape[0], all_iterate.shape[2]
    pieces, _, window, _ = parts.shape
    slices = fields.shape[0]
    own = window - 2 * reach
    my_coil = lax.axis_index("coil")
    row_base = rank_of(both) * own - reach

    barrier, arrivals = greet_all()
    sign = (2 * probe_bits[...] - 1).astype(f32)
    own_iterate[...] = iterate[:, 0].astype(bf16)
    own_fields[0:2] = sign[:, 0].astype(bf16)
    own_fields[2:4] = adjoint[:, 0].astype(bf16)
    edge = jnp.zeros((6, 8, depth), f32)
    padded[:, 0:8] = edge
    padded[:, height + reach : height + reach + 8] = edge
    weight = mask[...].astype(f32)
    weight = jnp.concatenate([weight, weight], axis=1)
    pl.semaphore_wait(barrier, arrivals)
    iterate_way.start()
    field_way.start()
    iterate_way.finish()

    real, imag = column(all_iterate, 0), column(all_iterate, 1)
    total_real, total_imag = coil_term(real, imag, 0, maps, kspace, weight, tables)
    field_way.finish()
    padded[0, reach : reach + height] = real
    padded[1, reach : reach + height] = imag
    for channel in range(4):
        padded[2 + channel, reach : reach + height] = column(all_fields, channel)
    for piece in range(slices):
        start = my_coil * (slices * own) + piece * own
        fields_send[piece] = padded[:, pl.ds(start, window), :].astype(bf16)
    window_way.start()
    for coil in range(1, maps.shape[0]):
        more_real, more_imag = coil_term(real, imag, coil, maps, kspace, weight, tables)
        total_real, total_imag = total_real + more_real, total_imag + more_imag
    padded[0, reach : reach + height] = total_real
    padded[1, reach : reach + height] = total_imag
    for piece in range(pieces):
        parts_send[piece] = padded[0:2, piece * own : piece * own + window, :].astype(bf16)
    part_way.start()

    def load(values):
        work[...] = values.reshape(work.shape)
        return jnp.concatenate([work[:, row, :] for row in range(window)], axis=1)

    def cut(values, before, after):
        return values[:, before * depth : values.shape[1] - after * depth]

    def inside(values, offset):
        blocks = []
        for row in range(values.shape[1] // depth):
            at = row_base + offset + row
            keep = jnp.where((at >= 0) & (at < height), 1.0, 0.0).astype(f32)
            blocks.append(values[:, row * depth : (row + 1) * depth] * keep)
        return jnp.concatenate(blocks, axis=1)

    def store(values):
        for row in range(own):
            rows_work[:, row, :] = values[:, row * depth : (row + 1) * depth]
        return rows_work[...].reshape(slices, 2, own, depth)

    build_rows(smalls[5], *in_band, last_t)
    build_rows(smalls[0], *in_band, first)
    build_rows(smalls[1], *mid_band, second)
    build_rows(smalls[4], *mid_band, second_t)
    build_taps(smalls[2], *out_band, last)
    build_taps(smalls[3], *out_band, first_t)
    window_way.finish()
    started = load(fields[:, 0:2].astype(f32))
    grads = []
    for field in range(2):
        probe = cut(load(fields[:, 2 + 2 * field : 4 + 2 * field].astype(f32)), 1, 1)
        grads.append(conv_in(probe, last_t, depth))
    part_way.finish()
    summed = parts[0:slices].astype(f32)
    for coil in range(1, coils):
        summed = summed + parts[coil * slices : (coil + 1) * slices].astype(f32)
    moved = load(-step_size * summed)
    relaxed = started + moved
    pre1 = conv_in(relaxed.astype(bf16).astype(f32), first, depth)
    sig1 = jax.nn.sigmoid(pre1)
    act1 = inside(pre1 * sig1, 1)
    slope1 = inside(cut(sig1 * (1.0 + pre1 * (1.0 - sig1)), 2, 2), 3)
    pre2 = conv_mid(act1, second, depth)
    sig2 = jax.nn.sigmoid(pre2)
    slope2 = inside(sig2 * (1.0 + pre2 * (1.0 - sig2)), 2)
    for field in range(2):
        grad1 = conv_mid(grads[field] * slope2, second_t, depth) * slope1
        pulled_send[field] = store(conv_out(grad1, first_t, depth)).astype(bf16)
        pulled_ways[field].start()
    act2 = inside(cut(pre2 * sig2, 1, 1), 3)
    delta_send[...] = store(conv_out(act2, last, depth) + cut(moved, reach, reach))
    delta_way.start()

    for field in range(2):
        pulled_ways[field].finish()
        real = column(all_fields, 2 * field) + column(pulled.at[field], 0)
        imag = column(all_fields, 2 * field + 1) + column(pulled.at[field], 1)
        total = None
        for coil in range(maps.shape[0]):
            term = coil_term(real, imag, coil, maps, None, weight, tables)
            total = term if total is None else (total[0] + term[0], total[1] + term[1])
        for part in range(2):
            for block in range(coils):
                at = block * rows
                sums_send[field, block, part] = total[part][at : at + rows].astype(bf16)
        sum_ways[field].start()

    delta_way.finish()
    for part in range(2):
        for piece in range(slices):
            at = piece * own
            changes[0, part, at : at + own] = delta[piece, part]
    for field in range(2):
        sum_ways[field].finish()
        for part in range(2):
            added = sums[field, 0, part].astype(f32)
            for block in range(1, coils):
                added = added + sums[field, block, part].astype(f32)
            mine = jnp.concatenate(
                [
                    pulled[field, my_coil * slices + piece, part].astype(f32)
                    for piece in range(slices)
                ],
                axis=0,
            )
            changes[1 + field, part] = mine - step_size * added


def on_device(coil_maps, kspace, sample_mask, iterate, probe_bits, loss_gradient, adjoint,
              kernel_first, kernel_second, kernel_last):
    height, depth = sample_mask.shape
    coils, slabs = lax.axis_size("coil"), lax.axis_size("slab")
    pieces = coils * slabs
    own = height // pieces
    window = own + 2 * reach
    rows = iterate.shape[2]
    tables = fourier_tables(height, depth, -1.0) + fourier_tables(height, depth, 1.0)
    kernels = (kernel_first, kernel_second, kernel_last)
    smalls = [small_kernel(kernel, form) for kernel, form in zip(kernels, ("in", "mid", "out"))]
    smalls += [
        small_kernel(transposed(kernel), form) for kernel, form in zip(kernels, ("out", "mid", "in"))
    ]
    constants = [
        constant
        for kernel, form in zip(kernels, ("in", "mid", "out"))
        for constant in band_constants(kernel, slabs, form)
    ]
    hidden, channels = kernel_second.shape[0] * slabs, kernel_first.shape[1] * slabs
    buffers = [
        ((6, height + 2 * reach + 8, depth), f32),
        ((2 * slabs, window, depth), f32),
        ((2 * slabs, own, depth), f32),
        ((2, rows, depth), bf16),
        ((4, rows, depth), bf16),
        ((coils, 2, rows, depth), bf16),
        ((coils, 4, rows, depth), bf16),
        ((pieces, 2, window, depth), bf16),
        ((pieces, 2, window, depth), bf16),
        ((slabs, 6, window, depth), bf16),
        ((slabs, 6, window, depth), bf16),
        ((slabs, 2, own, depth), f32),
        ((slabs, 2, own, depth), f32),
        ((2, slabs, 2, own, depth), bf16),
        ((2, pieces, 2, own, depth), bf16),
        ((2, coils, 2, rows, depth), bf16),
        ((2, coils, 2, rows, depth), bf16),
        ((1, hidden, 9 * channels), bf16),
        ((3, hidden, 3 * hidden), bf16),
        ((9, channels, hidden), bf16),
        ((9, channels, hidden), bf16),
        ((3, hidden, 3 * hidden), bf16),
        ((1, hidden, 9 * channels), bf16),
    ]
    ways = (coils, coils, slabs, pieces, slabs, pieces, pieces, coils, coils)
    changes = pl.pallas_call(
        step_kernel,
        out_shape=jax.ShapeDtypeStruct((3, 2, rows, depth), f32),
        in_specs=[vmem] * 27,
        out_specs=vmem,
        scratch_shapes=[pltpu.VMEM(shape, kind) for shape, kind in buffers]
        + [pltpu.SemaphoreType.DMA((size,)) for size in ways for _ in range(2)],
        compiler_params=pltpu.CompilerParams(collective_id=0, has_side_effects=True),
    )(coil_maps, kspace, sample_mask, iterate, probe_bits, adjoint, *tables, *smalls, *constants)
    changes = changes[:, :, None]
    sign = (2 * probe_bits - 1).astype(f32)
    return iterate + changes[0], sign + changes[1], loss_gradient + (adjoint + changes[2])


def solution(mesh):
    split_coils = P("coil", None, "slab", None, None)
    image = P(None, "slab", "coil", None)
    return jax.shard_map(
        on_device,
        mesh=mesh,
        in_specs=(split_coils, split_coils, P(), image, image, image, image, P(), P(), P()),
        out_specs=(image, image, image),
        check_vma=False,
    )
```
